256 devices in a mesh: seq: 16 (over z_lo, x), mp: 16 (over y, z_hi, core).
Axes of the slice: x: 4, y: 4, z: 8 (z_hi: 2, z_lo: 4; z = z_hi * 4 + z_lo), core: 2. Of those that a mesh axis runs over, the one named last changes fastest.
Arguments:
- inputs: bfloat16 [8192, 7168], P('seq')
- norm_gain: float32 [7168], replicated, may hold values from 0.1 to 1.9
- qkv_weight: bfloat16 [7168, 3, 3584], P('seq', None, 'mp'), may hold values from -0.0625 to 0.0625
- adapter_down: bfloat16 [7168, 128], P('seq'), may hold values from -0.0625 to 0.0625
- adapter_up: bfloat16 [3, 128, 3584], P(None, None, 'mp'), may hold values from -0.5 to 0.5
- out_weight: bfloat16 [3584, 3584], P('mp', 'seq'), may hold values from -0.5 to 0.5
- cache_keys: bfloat16 [32, 256, 3584], P('seq', None, 'mp')
- cache_values: bfloat16 [32, 256, 3584], P('seq', None, 'mp'), may hold values from -6 to 6
- cache_lengths: int32 [4], replicated, may hold values from 1 to 2048, 5120 in all
- block_perm: int32 [32], replicated, may hold values from 0 to 31, each once
Outputs:
- block_out: bfloat16 [8192, 3584], P('seq', 'mp')
The draws below stay inside these ranges and needn't reach their ends.
Inputs may be any that keep to these rules, and one draw needn't show every extreme that they name: `cache_lengths`: each request has at least one cached position, and some request fills all of its 8 blocks. `block_perm`: each logical block appears once.
All inputs are finite; a program needn't handle non-finite values.
Results may differ from the reference program's by a relative error of at most 0.025.
Values may be sent and summed in bfloat16 or wider, within the bound.
A program may use at most 192 MiB of HBM per device.

```python
import math
import jax
import jax.numpy as jnp
import numpy as np
from jax import lax

D = 3584
D_IN = 7168
HEADS = 16
HD = 224
RANK = 128
REQS = 4
QLEN = 2048
BLK = 256
TOKENS = 8192
NBLK_ALL = 32
MAXB = 8


def draw_inputs(key, part):
    base_key, row_key, col_key = jax.random.split(key, 3)
    array_shape = (TOKENS, D_IN)
    base_draw = jax.random.normal(base_key, array_shape, jnp.float32)
    row_scale = jnp.exp(jax.random.uniform(row_key, (TOKENS, 1), jnp.float32, 0.0, math.log(10.0)))
    col_scale = jnp.exp(jax.random.uniform(col_key, (1, D_IN), jnp.float32, 0.0, math.log(10.0)))
    return (base_draw * row_scale * col_scale).astype(jnp.bfloat16)


def draw_cache_keys(key, part):
    base_key = jax.random.fold_in(key, 0)
    array_shape = (NBLK_ALL, BLK, HEADS * HD)
    base_draw = jax.random.normal(base_key, array_shape, jnp.float32)
    return base_draw.astype(jnp.bfloat16)


def strengthened(drawn, rng, source, target, shards_of, factor):
    owner, partner = [(jnp.arange(drawn.shape[dim]) // (drawn.shape[dim] // shards_of)).reshape([-1 if axis == dim else 1 for axis in range(drawn.ndim)]) for dim in (source, target)]
    chosen = jax.random.permutation(rng, shards_of)[partner]
    strong = (owner == chosen) | (owner == (partner + shards_of // 2) % shards_of)
    return jnp.where(strong, factor * drawn, drawn)


def block_scale(stream_key, dims, cuts, smallest, top_value):
    def one(position, parts):
        steps = jax.random.uniform(jax.random.fold_in(jax.random.fold_in(stream_key, 6), position), (parts,), jnp.float32, smallest / len(cuts), top_value / len(cuts))
        return jnp.repeat(jnp.exp(steps), dims[position] // parts).reshape((-1,) + (1,) * (len(dims) - position - 1))

    loudness = one(*cuts[0])
    for cut in cuts[1:]:
        loudness = loudness * one(*cut)
    return loudness


def profile(number_of, total, most, skew):
    weights = [(1 << 20) // math.isqrt(grade ** skew) + 1 for grade in range(2, number_of + 1)]
    surplus, counts = total - most - (number_of - 1), [1] * (number_of - 1)
    while surplus > 0:
        movable = [i for i in range(number_of - 1) if counts[i] < most]
        mass, budget = sum([weights[i] for i in movable]), surplus
        for i in movable:
            more = min(most - counts[i], max(1, budget * weights[i] // mass), surplus)
            counts[i] = counts[i] + more
            surplus = surplus - more
    return np.array([most] + counts)


def ragged(rng, number_of, total, bound, skew):
    if number_of == 2:
        one = jax.random.randint(rng, (), max(1, total - bound), min(bound, total - 1) + 1)
        return jnp.stack([one, total - one])
    tallies = jnp.asarray(profile(number_of, total, bound, skew), jnp.int32)
    couples = (number_of - 1) // 2
    source_of, sink = tallies[1:1 + 2 * couples:2], tallies[2:2 + 2 * couples:2]
    slack = jnp.minimum(source_of - 1, bound - sink)
    moved = jax.random.randint(jax.random.fold_in(rng, 1), (couples,), 0, 1 << 20) % (slack + 1)
    tallies = tallies.at[1:1 + 2 * couples:2].set(source_of - moved).at[2:2 + 2 * couples:2].set(sink + moved)
    return tallies[jax.random.permutation(jax.random.fold_in(rng, 2), number_of)]


def centred(stream_key, shape, deviation, reach, pieces=(), kind=jnp.bfloat16):
    result = jax.random.normal(stream_key, shape, jnp.float32) * deviation
    if len(pieces) > 0:
        result = block_scale(stream_key, shape, pieces, -0.22, 0.18) * result
    return jnp.clip(result, min=-reach, max=reach).astype(kind)


def heavy_noise(rng, dims, deviation, bound, pieces, heavy, kind=jnp.bfloat16):
    entries = deviation * jax.random.normal(rng, dims, jnp.float32)
    if pieces:
        entries = entries * block_scale(rng, dims, pieces, -0.22, 0.18)
    return jnp.clip(strengthened(entries, jax.random.fold_in(rng, 3), *heavy), -bound, bound).astype(kind)


def setup_inputs(seed: int = 0) -> dict:
    keys = jax.random.split(jax.random.key(seed), 11)
    return {
        "inputs": draw_inputs(jax.random.fold_in(keys[10], 71), 0),
        "norm_gain": jnp.clip(1.0 + 0.18 * jax.random.normal(keys[1], (D_IN,), jnp.float32), 0.1, 1.9),
        "qkv_weight": centred(keys[2], (D_IN, 3, HEADS * HD), D_IN ** -0.5, 0.0625, ((0, 16), (2, 16))),
        "adapter_down": centred(keys[3], (D_IN, RANK), D_IN ** -0.5, 0.0625, ((0, 16),)),
        "adapter_up": centred(keys[4], (3, RANK, HEADS * HD), RANK ** -0.5, 0.5, ((2, 16),)),
        "out_weight": heavy_noise(keys[5], (HEADS * HD, D), HD ** -0.5, 0.5, ((0, 16), (1, 16)), (0, 1, 16, 2.0)),
        "cache_keys": draw_cache_keys(jax.random.fold_in(keys[10], 71), 0),
        "cache_values": centred(keys[7], (NBLK_ALL, BLK, HEADS * HD), 1.0, 6.0, ((0, 16), (2, 16))),
        "cache_lengths": ragged(keys[8], REQS, MAXB * BLK * REQS * 5 // 8, MAXB * BLK, 2).astype(jnp.int32),
        "block_perm": jax.random.permutation(keys[9], NBLK_ALL).astype(jnp.int32),
    }


lowest = -1e+30

def reference(inputs, norm_gain, qkv_weight, adapter_down, adapter_up, out_weight, cache_keys, cache_values, cache_lengths, block_perm):
    widened = inputs.astype(jnp.float32)
    normed = (widened * lax.rsqrt(lax.optimization_barrier(jnp.mean(widened * widened, axis=-1, keepdims=True)) + 1e-05) * norm_gain).astype(jnp.bfloat16)
    low_rank = jnp.dot(normed, adapter_down, preferred_element_type=jnp.float32).astype(jnp.bfloat16)
    main_part = jnp.dot(normed, qkv_weight.reshape(D_IN, 3 * HEADS * HD), preferred_element_type=jnp.float32).reshape(TOKENS, 3, HEADS * HD)
    extra = jnp.einsum('tr,krc->tkc', low_rank.astype(jnp.float32), adapter_up.astype(jnp.float32))
    projected = (main_part + extra).astype(jnp.bfloat16)
    max_blocks = NBLK_ALL // REQS
    cache_span = max_blocks * BLK
    inverse = jnp.zeros((NBLK_ALL,), jnp.int32).at[block_perm].set(jnp.arange(NBLK_ALL, dtype=jnp.int32))
    logical_keys = cache_keys[inverse].reshape(REQS, cache_span, HEADS, HD)
    logical_values = cache_values[inverse].reshape(REQS, cache_span, HEADS, HD)
    scale = HD ** (-0.5)

    def one_slot(slot_index):
        request = slot_index
        length = cache_lengths[request]
        rows = lax.dynamic_slice_in_dim(projected, (slot_index * QLEN).astype(jnp.int32), QLEN, 0)
        key_rows = jnp.concatenate([logical_keys[request], rows[:, 1].reshape(QLEN, HEADS, HD)], axis=0)
        value_rows = jnp.concatenate([logical_values[request], rows[:, 2].reshape(QLEN, HEADS, HD)], axis=0)
        cache_ids = jnp.arange(cache_span, dtype=jnp.int32)
        query_pos = length + jnp.arange(QLEN, dtype=jnp.int32)
        key_pos = jnp.concatenate([cache_ids, query_pos])
        key_live = jnp.concatenate([cache_ids < length, jnp.ones((QLEN,), dtype=bool)])
        visible = key_live[None, :] & (key_pos[None, :] <= query_pos[:, None])
        query_rows = rows[:, 0].reshape(QLEN, HEADS, HD)

        def one_head(operands):
            head_queries, head_keys, head_values = operands
            scores = jnp.dot(head_queries, head_keys.T, preferred_element_type=jnp.float32) * scale
            scores = jnp.where(visible, scores, lowest)
            largest = lax.optimization_barrier(jnp.max(scores, axis=-1, keepdims=True))
            weights = jnp.where(visible, jnp.exp(scores - largest), 0.0)
            weight_sum = lax.optimization_barrier(jnp.sum(weights, axis=-1, keepdims=True))
            mixed = jnp.dot(weights.astype(jnp.bfloat16), head_values, preferred_element_type=jnp.float32)
            return (mixed / weight_sum).astype(jnp.bfloat16)
        per_head = lax.map(one_head, (query_rows.transpose(1, 0, 2), key_rows.transpose(1, 0, 2), value_rows.transpose(1, 0, 2)))
        return per_head.transpose(1, 0, 2).reshape(QLEN, HEADS * HD)
    attended = lax.map(one_slot, jnp.arange(REQS, dtype=jnp.int32)).reshape(TOKENS, HEADS * HD)
    return jnp.dot(attended, out_weight, preferred_element_type=jnp.float32).astype(jnp.bfloat16)
```

```python
import functools

import jax
import jax.numpy as jnp
from jax import lax
from jax.experimental import pallas as pl
from jax.experimental.pallas import tpu as pltpu
from jax.sharding import PartitionSpec as P

HD = 224
REQS = 4
NX = 4
NZ = 4
EPS = 1e-05
LOWEST = -1e30
VMEM_LIMIT = 60 * 1024 * 1024
F32 = jnp.float32
BF16 = jnp.bfloat16


def seq_dev(z, x):
    return {"seq": z * NX + x}


def mp_dev(y, zh, core):
    return {"mp": y * 4 + zh * 2 + core}


def greet(devices, conditions):
    barrier = pltpu.get_barrier_semaphore()
    count = jnp.int32(0)
    for device, condition in zip(devices, conditions):
        if condition is None:
            pl.semaphore_signal(barrier, inc=1, device_id=device, device_id_type=pl.DeviceIdType.MESH)
            count = count + 1
        else:

            @pl.when(condition)
            def _():
                pl.semaphore_signal(barrier, inc=1, device_id=device, device_id_type=pl.DeviceIdType.MESH)

            count = count + condition.astype(jnp.int32)
    pl.semaphore_wait(barrier, count)


def remote(src, dst, send_sem, recv_sem, device):
    return pltpu.make_async_remote_copy(
        src_ref=src, dst_ref=dst, send_sem=send_sem, recv_sem=recv_sem,
        device_id=device, device_id_type=pl.DeviceIdType.MESH,
    )


def gather_kernel(
    table, x_hbm, gain_ref, w_hbm, ck_hbm, cv_hbm, ow_hbm,
    proj_ref, kv_ref, og_ref,
    xin, wall, row_kv, up, down, acc,
    load_sem, x_sem, w_recv, w_send, zw_send, o_recv, o_send, zo_send,
    c_recv, c_send, m_recv, m_send, f_recv, f_send,
):
    me = lax.axis_index("seq")
    z, x = me // NX, me % NX
    right, left, opp = (x + 1) % NX, (x + 3) % NX, (x + 2) % NX
    shard = w_hbm.shape[1]
    tok = xin.shape[0]
    half = shard // 2
    o_rows = og_ref.shape[1]
    o_half = o_rows // 2

    def wrows(s, part):
        return wall.at[:, pl.ds(pl.multiple_of(s * shard + part * half, 16), half), :]

    def orows(s, part):
        return og_ref.at[s, pl.ds(part * o_half, o_half), :]

    loads = [
        pltpu.make_async_copy(ck_hbm, row_kv.at[0, x], load_sem.at[0]),
        pltpu.make_async_copy(cv_hbm, row_kv.at[1, x], load_sem.at[1]),
        pltpu.make_async_copy(
            w_hbm, wall.at[:, pl.ds(pl.multiple_of(me * shard, 16), shard), :], load_sem.at[2]
        ),
        pltpu.make_async_copy(ow_hbm, og_ref.at[me], load_sem.at[3]),
        pltpu.make_async_copy(x_hbm, xin, x_sem),
    ]
    for load in loads:
        load.start()

    greet(
        [seq_dev(z, right), seq_dev(z, left), seq_dev(jnp.minimum(z + 1, NZ - 1), x), seq_dev(jnp.maximum(z - 1, 0), x)],
        [None, None, z < NZ - 1, z > 0],
    )

    def c_copy(kind, xs, way):
        target = right if way == 0 else left
        return remote(
            row_kv.at[kind, xs], row_kv.at[kind, xs],
            c_send.at[kind, way, 0 if xs is x else 1], c_recv.at[kind, xs], seq_dev(z, target),
        )

    loads[0].wait()
    loads[1].wait()
    for kind in (0, 1):
        for way in (0, 1):
            c_copy(kind, x, way).start()

    loads[2].wait()

    def order(j):
        zz = jnp.where(z < 2, z, 3 - z)
        o = zz if j == 0 else (1 - zz if j == 1 else j)
        return jnp.where(z < 2, o, 3 - o)

    def w_copy(s, part, send, device):
        return remote(wrows(s, part), wrows(s, part), send, w_recv.at[s, part], device)

    def o_copy(s, part, send, device):
        return remote(orows(s, part), orows(s, part), send, o_recv.at[s, part], device)

    def z_start(copy, sends, j):
        zs = order(j)
        s = zs * NX + x
        for way in (0, 1):
            zt = z + 1 if way == 0 else z - 1
            inside = (zt >= 0) & (zt < NZ)
            if j > 0:
                inside = inside & ((zs < z) if way == 0 else (zs > z))

            @pl.when(inside)
            def _():
                for part in (0, 1):
                    copy(s, part, sends.at[j, part, way], seq_dev(zt, x)).start()

    def z_finish(copy, sends):
        for j in range(NZ):
            zs = order(j)
            s = zs * NX + x
            for way in (0, 1):
                zt = z + 1 if way == 0 else z - 1
                inside = (zt >= 0) & (zt < NZ)
                if j > 0:
                    inside = inside & ((zs < z) if way == 0 else (zs > z))

                @pl.when(inside)
                def _():
                    for part in (0, 1):
                        copy(s, part, sends.at[j, part, way], seq_dev(zt, x)).wait_send()

    def z_arrive(copy, sends, j):
        s = order(j) * NX + x
        for part in (0, 1):
            copy(s, part, sends.at[j, part, 0], seq_dev(z, right)).wait_recv()

    def x_own(copy, sends, j):
        s = order(j) * NX + x
        for part in (0, 1):
            copy(s, part, sends.at[j, part, 0], seq_dev(z, right)).start()
            copy(s, part, sends.at[j, part, 1], seq_dev(z, left)).start()

    def x_near(copy, sends, j):
        row = order(j) * NX
        for part in (0, 1):
            source, target = (left, right) if part == 0 else (right, left)
            other = right if part == 0 else left
            copy(row + source, part, sends.at[j, part, 2], seq_dev(z, target)).wait_recv()
            copy(row + source, part, sends.at[j, part, 2], seq_dev(z, target)).start()
        for part in (0, 1):
            other = right if part == 0 else left
            copy(row + other, part, sends.at[j, part, 2], seq_dev(z, right)).wait_recv()

    def x_far(copy, sends, j):
        row = order(j) * NX
        for part in (0, 1):
            copy(row + opp, part, sends.at[j, part, 2], seq_dev(z, right)).wait_recv()

    def x_finish(copy, sends):
        for j in range(NZ):
            row = order(j) * NX
            for part in (0, 1):
                copy(row + x, part, sends.at[j, part, 0], seq_dev(z, right)).wait_send()
                copy(row + x, part, sends.at[j, part, 1], seq_dev(z, left)).wait_send()
                source = left if part == 0 else right
                copy(row + source, part, sends.at[j, part, 2], seq_dev(z, right)).wait_send()

    z_start(w_copy, zw_send, 0)

    loads[4].wait()

    @pl.loop(0, tok // 16)
    def _(i):
        rows = pl.ds(pl.multiple_of(i * 16, 16), 16)
        wide = xin[rows, :].astype(F32)
        mean = jnp.mean(wide * wide, axis=-1, keepdims=True)
        xin[rows, :] = (wide * lax.rsqrt(mean + EPS) * gain_ref[...]).astype(BF16)

    for kind in (0, 1):
        source = left if kind == 0 else right
        c_copy(kind, source, kind).wait_recv()
        c_copy(kind, source, kind).start()
    x_own(w_copy, w_send, 0)
    for kind in (0, 1):
        c_copy(kind, right if kind == 0 else left, 0).wait_recv()
    for kind in (0, 1):
        c_copy(kind, opp, 0).wait_recv()

    def held(kind, d, i):
        return row_kv[kind, table[8 + 2 * d + i] // 2, table[8 + 2 * d + i] % 2]

    def message(buffer, way, d, kind):
        return remote(
            buffer.at[d, kind], buffer.at[d, kind], m_send.at[way, d, kind], m_recv.at[way, d, kind],
            seq_dev(jnp.clip(z + 1 - 2 * way, 0, NZ - 1), x),
        )

    def relay(way, hop):
        buffer = up if way == 0 else down
        here = hop if way == 0 else NZ - 1 - hop

        @pl.when(z == here)
        def _():
            passing = range(NZ - 1, here, -1) if way == 0 else range(0, here)
            for d in passing:
                for kind in (0, 1):
                    if hop > 0:
                        message(buffer, way, d, kind).wait_recv()
                    for i in (0, 1):
                        if hop == 0:
                            buffer[d, kind, i] = held(kind, d, i)
                        else:
                            buffer[d, kind, i] = jnp.where(
                                table[2 * d + i] == here, held(kind, d, i), buffer[d, kind, i]
                            )
                    message(buffer, way, d, kind).start()
            if hop > 0:
                for kind in (0, 1):
                    message(buffer, way, here, kind).wait_recv()

    def relay_finish(way):
        buffer = up if way == 0 else down
        for here in range(NZ):
            passing = range(NZ - 1, here, -1) if way == 0 else range(0, here)

            @pl.when(z == here)
            def _():
                for d in passing:
                    for kind in (0, 1):
                        message(buffer, way, d, kind).wait_send()

    def multiply(j):
        zs = order(j)
        width = NX * shard
        span = pl.ds(pl.multiple_of(zs * width, 128), width)

        @pl.loop(0, tok // 128)
        def _(i):
            rows = pl.ds(pl.multiple_of(i * 128, 128), 128)
            for k in range(3):
                got = jnp.dot(
                    xin[rows, span], wall[k, pl.ds(pl.multiple_of(zs * width, 16), width), :],
                    preferred_element_type=F32,
                )
                if j == 0:
                    acc[k, rows, :] = got
                elif j < NZ - 1:
                    acc[k, rows, :] += got
                else:
                    proj_ref[k, rows, :] = (acc[k, rows, :] + got).astype(BF16)

    relay(0, 0)
    relay(1, 0)
    z_arrive(w_copy, zw_send, 1)
    z_start(w_copy, zw_send, 1)
    x_own(w_copy, w_send, 1)
    x_near(w_copy, w_send, 0)
    relay(0, 1)
    relay(1, 1)
    z_arrive(w_copy, zw_send, 2)
    z_start(w_copy, zw_send, 2)
    x_own(w_copy, w_send, 2)
    loads[3].wait()
    z_start(o_copy, zo_send, 0)
    x_far(w_copy, w_send, 0)
    multiply(0)
    x_near(w_copy, w_send, 1)
    relay(0, 2)
    relay(1, 2)
    z_arrive(w_copy, zw_send, 3)
    z_start(w_copy, zw_send, 3)
    x_own(w_copy, w_send, 3)
    x_far(w_copy, w_send, 1)
    multiply(1)
    x_near(w_copy, w_send, 2)
    relay(0, 3)
    relay(1, 3)

    for kind in (0, 1):
        for i in (0, 1):
            low = up[z, kind, i]
            high = down[z, kind, i]
            origin = table[2 * z + i]
            kv_ref[kind, 2 * x + i] = jnp.where(
                origin == z, held(kind, z, i), jnp.where(origin < z, low, high)
            )

    def f_copy(kind, xs, slot, target):
        ref = kv_ref.at[kind, pl.ds(2 * xs, 2)]
        return remote(ref, ref, f_send.at[kind, slot], f_recv.at[kind, xs], seq_dev(z, target))

    for kind in (0, 1):
        f_copy(kind, x, 0, right).start()
        f_copy(kind, x, 1, left).start()
    x_own(o_copy, o_send, 0)
    for j in (1, 2, 3):
        z_arrive(o_copy, zo_send, j)
        z_start(o_copy, zo_send, j)
        x_own(o_copy, o_send, j)
    x_far(w_copy, w_send, 2)
    multiply(2)
    x_near(w_copy, w_send, 3)
    for kind in (0, 1):
        source, target = (left, right) if kind == 0 else (right, left)
        f_copy(kind, source, 2, target).wait_recv()
        f_copy(kind, source, 2, target).start()
    for j in range(NZ):
        x_near(o_copy, o_send, j)
    x_far(w_copy, w_send, 3)
    multiply(3)
    for kind in (0, 1):
        f_copy(kind, right if kind == 0 else left, 2, right).wait_recv()
        f_copy(kind, opp, 2, right).wait_recv()
    for j in range(NZ):
        x_far(o_copy, o_send, j)

    for kind in (0, 1):
        for way in (0, 1):
            c_copy(kind, x, way).wait_send()
        c_copy(kind, left if kind == 0 else right, kind).wait_send()
        for slot in range(3):
            f_copy(kind, x, slot, right).wait_send()
    relay_finish(0)
    relay_finish(1)
    z_finish(w_copy, zw_send)
    x_finish(w_copy, w_send)
    z_finish(o_copy, zo_send)
    x_finish(o_copy, o_send)


def attend_kernel(
    length, proj_ref, kv_ref, og_ref, out_ref,
    near, top, total, mixed, attended, parts, mates, ring, sums,
    k_recv, k_send, a_recv, a_send, y_recv, y_send, h_recv, h_send,
):
    me = lax.axis_index("seq")
    mp = lax.axis_index("mp")
    z, x = me // NX, me % NX
    right, left, opp = (x + 1) % NX, (x + 3) % NX, (x + 2) % NX
    y, zh, core = mp // 4, (mp // 2) % 2, mp % 2
    y_up, y_dn, y_opp = (y + 1) % 4, (y + 3) % 4, (y + 2) % 4
    tok = proj_ref.shape[1]

    greet(
        [seq_dev(z, right), seq_dev(z, left), mp_dev(y, zh, 1 - core), mp_dev(y_up, zh, core), mp_dev(y_dn, zh, core), mp_dev(y, 1 - zh, core)],
        [None] * 6,
    )

    def k_copy(kind, xs, slot, target):
        src = proj_ref.at[1 + kind] if xs is x else near.at[kind, xs]
        return remote(src, near.at[kind, xs], k_send.at[kind, slot], k_recv.at[kind, xs], seq_dev(z, target))

    for kind in (0, 1):
        k_copy(kind, x, 0, right).start()
        k_copy(kind, x, 1, left).start()

    scale = HD ** (-0.5)

    def update(keys, values, mask, first=False):
        scores = lax.dot_general(
            proj_ref[0], keys, (((1,), (1,)), ((), ())), preferred_element_type=F32
        ) * scale
        if mask is not None:
            scores = jnp.where(mask, scores, LOWEST)
        largest = jnp.max(scores, axis=-1, keepdims=True)
        if not first:
            largest = jnp.maximum(largest, top[...])
        weights = jnp.exp(scores - largest)
        weight_sum = jnp.sum(weights, axis=-1, keepdims=True)
        got = jnp.dot(weights.astype(BF16), values, preferred_element_type=F32)
        if first:
            total[...] = weight_sum
            mixed[...] = got
        else:
            fade = jnp.exp(top[...] - largest)
            total[...] = total[...] * fade + weight_sum
            mixed[...] = mixed[...] * fade + got
        top[...] = largest

    columns = lax.broadcasted_iota(jnp.int32, (tok, 512), 1)
    update(
        kv_ref[0, 0:2].reshape(512, HD), kv_ref[1, 0:2].reshape(512, HD), columns < length[0], True
    )

    @pl.loop(1, 4)
    def _(c):
        two = pl.ds(2 * c, 2)
        ids = lax.broadcasted_iota(jnp.int32, (tok, 512), 1) + c * 512
        update(kv_ref[0, two].reshape(512, HD), kv_ref[1, two].reshape(512, HD), ids < length[0])

    rows = lax.broadcasted_iota(jnp.int32, (tok, tok), 0)
    update(proj_ref[1], proj_ref[2], columns <= rows)

    for kind in (0, 1):
        source, target = (left, right) if kind == 0 else (right, left)
        k_copy(kind, source, 2, target).wait_recv()
        k_copy(kind, source, 2, target).start()
    for kind in (0, 1):
        k_copy(kind, right if kind == 0 else left, 2, right).wait_recv()

    @pl.when(x > 0)
    def _():
        update(near[0, left], near[1, left], None)

    @pl.when(x == NX - 1)
    def _():
        update(near[0, right], near[1, right], None)

    for kind in (0, 1):
        k_copy(kind, opp, 2, right).wait_recv()

    @pl.when(x > 1)
    def _():
        update(near[0, opp], near[1, opp], None)

    attended[...] = (mixed[...] / total[...]).astype(BF16)

    @pl.loop(0, 8)
    def _(c):
        parts[c] = jnp.dot(
            attended[...], og_ref[2 * c + 1 - core], preferred_element_type=F32
        ).astype(BF16)

    mate = remote(parts, mates, a_send, a_recv, mp_dev(y, zh, 1 - core))
    mate.start()

    @pl.loop(0, 8)
    def _(c):
        sums[c] = jnp.dot(attended[...], og_ref[2 * c + core], preferred_element_type=F32).astype(BF16)

    mate.wait_recv()

    @pl.loop(0, 8)
    def _(c):
        sums[c] = (sums[c].astype(F32) + mates[c].astype(F32)).astype(BF16)

    def far(way):
        target = y_up if way == 0 else y_dn
        return remote(
            sums.at[2 * y_opp + way], ring.at[way, 0], y_send.at[way, 0], y_recv.at[way, 0],
            mp_dev(target, zh, core),
        )

    def close(way, h):
        target = y_up if way == 0 else y_dn
        return remote(
            sums.at[2 * target + h], ring.at[way, 1 + h], y_send.at[way, 1 + h], y_recv.at[way, 1 + h],
            mp_dev(target, zh, core),
        )

    far(0).start()
    far(1).start()
    for way in (0, 1):
        close(way, 1 - way).start()
    for way in (0, 1):
        target = y_up if way == 0 else y_dn
        far(way).wait_recv()
        sums[2 * target + way] = (
            sums[2 * target + way].astype(F32) + ring[way, 0].astype(F32)
        ).astype(BF16)
        close(way, way).start()
    for way in (0, 1):
        for h in (0, 1):
            close(way, h).wait_recv()

    def chunk(h):
        return sums[2 * y + h].astype(F32) + ring[0, 1 + h].astype(F32) + ring[1, 1 + h].astype(F32)

    attended[...] = jnp.where(zh == 0, chunk(1), chunk(0)).astype(BF16)
    last = remote(attended, near.at[0, x], h_send, h_recv, mp_dev(y, 1 - zh, core))
    last.start()
    mine = jnp.where(zh == 0, chunk(0), chunk(1))
    last.wait_recv()
    out_ref[...] = (mine + near[0, x].astype(F32)).astype(BF16)

    for kind in (0, 1):
        for slot in range(3):
            k_copy(kind, x, slot, right).wait_send()
    mate.wait_send()
    for way in (0, 1):
        far(way).wait_send()
        close(way, 0).wait_send()
        close(way, 1).wait_send()
    last.wait_send()


def vmem():
    return pl.BlockSpec(memory_space=pltpu.VMEM)


def smem():
    return pl.BlockSpec(memory_space=pltpu.SMEM)


def hbm():
    return pl.BlockSpec(memory_space=pl.ANY)


def per_device(
    inputs, norm_gain, qkv_weight, adapter_down, adapter_up, out_weight,
    cache_keys, cache_values, cache_lengths, block_perm,
):
    tok, d_in = inputs.shape
    shard = qkv_weight.shape[0]
    blk = cache_keys.shape[1]
    dma = pltpu.SemaphoreType.DMA
    me = lax.axis_index("seq")
    z, x = me // NX, me % NX

    folded = (
        qkv_weight.transpose(1, 0, 2).astype(F32)
        + jnp.einsum("rj,kjc->krc", adapter_down, adapter_up, preferred_element_type=F32)
    ).astype(BF16)

    logical = jnp.arange(NZ, dtype=jnp.int32)[:, None] * 8 + 2 * x + jnp.arange(2, dtype=jnp.int32)[None, :]
    count = block_perm.shape[0]
    hits = block_perm[None, :] == logical.reshape(-1)[:, None]
    place = jnp.sum(jnp.where(hits, jnp.arange(count, dtype=jnp.int32)[None, :], 0), axis=-1)
    table = jnp.concatenate([place // 8, place % 8]).astype(jnp.int32)
    length = jnp.sum(
        jnp.where(jnp.arange(REQS, dtype=jnp.int32) == z, cache_lengths, 0)
    ).reshape(1)

    proj, kv, og = pl.pallas_call(
        gather_kernel,
        out_shape=(
            jax.ShapeDtypeStruct((3, tok, HD), BF16),
            jax.ShapeDtypeStruct((2, 8, blk, HD), BF16),
            jax.ShapeDtypeStruct((16, HD, HD), BF16),
        ),
        in_specs=[smem(), hbm(), vmem(), hbm(), hbm(), hbm(), hbm()],
        out_specs=(vmem(), vmem(), vmem()),
        scratch_shapes=[
            pltpu.VMEM((tok, d_in), BF16),
            pltpu.VMEM((3, d_in, HD), BF16),
            pltpu.VMEM((2, NX, 2, blk, HD), BF16),
            pltpu.VMEM((NZ, 2, 2, blk, HD), BF16),
            pltpu.VMEM((NZ, 2, 2, blk, HD), BF16),
            pltpu.VMEM((3, tok, HD), F32),
            dma((4,)), dma,
            dma((16, 2)), dma((4, 2, 3)), dma((4, 2, 2)),
            dma((16, 2)), dma((4, 2, 3)), dma((4, 2, 2)),
            dma((2, 4)), dma((2, 2, 2)),
            dma((2, 4, 2)), dma((2, 4, 2)),
            dma((2, 4)), dma((2, 3)),
        ],
        compiler_params=pltpu.CompilerParams(
            collective_id=0, has_side_effects=True, vmem_limit_bytes=VMEM_LIMIT
        ),
        name="gather",
    )(table, inputs, norm_gain.reshape(1, d_in), folded, cache_keys, cache_values, out_weight)

    return pl.pallas_call(
        attend_kernel,
        out_shape=jax.ShapeDtypeStruct((tok, HD), BF16),
        in_specs=[smem(), vmem(), vmem(), vmem()],
        out_specs=vmem(),
        scratch_shapes=[
            pltpu.VMEM((2, NX, tok, HD), BF16),
            pltpu.VMEM((tok, 1), F32),
            pltpu.VMEM((tok, 1), F32),
            pltpu.VMEM((tok, HD), F32),
            pltpu.VMEM((tok, HD), BF16),
            pltpu.VMEM((8, tok, HD), BF16),
            pltpu.VMEM((8, tok, HD), BF16),
            pltpu.VMEM((2, 3, tok, HD), BF16),
            pltpu.VMEM((8, tok, HD), BF16),
            dma((2, 4)), dma((2, 3)),
            dma, dma,
            dma((2, 3)), dma((2, 3)),
            dma, dma,
        ],
        compiler_params=pltpu.CompilerParams(
            collective_id=1, has_side_effects=True, vmem_limit_bytes=VMEM_LIMIT
        ),
        name="attend",
    )(length, proj, kv, og)


def solution(mesh):
    in_specs = (
        P("seq", None), P(), P("seq", None, "mp"), P("seq", None), P(None, None, "mp"),
        P("mp", "seq"), P("seq", None, "mp"), P("seq", None, "mp"), P(), P(),
    )
    return jax.shard_map(
        per_device, mesh=mesh, in_specs=in_specs, out_specs=P("seq", "mp"), check_vma=False
    )
```

```python
import functools

import jax
import jax.numpy as jnp
from jax import lax
from jax.experimental import pallas as pl
from jax.experimental.pallas import tpu as pltpu
from jax.sharding import PartitionSpec as P

HD = 224
REQS = 4
NX = 4
NZ = 4
EPS = 1e-05
LOWEST = -1e30
VMEM_LIMIT = 60 * 1024 * 1024
F32 = jnp.float32
BF16 = jnp.bfloat16


def seq_dev(z, x):
    return {"seq": z * NX + x}


def mp_dev(y, zh, core):
    return {"mp": y * 4 + zh * 2 + core}


def greet(devices, conditions):
    barrier = pltpu.get_barrier_semaphore()
    count = jnp.int32(0)
    for device, condition in zip(devices, conditions):
        if condition is None:
            pl.semaphore_signal(barrier, inc=1, device_id=device, device_id_type=pl.DeviceIdType.MESH)
            count = count + 1
        else:

            @pl.when(condition)
            def _():
                pl.semaphore_signal(barrier, inc=1, device_id=device, device_id_type=pl.DeviceIdType.MESH)

            count = count + condition.astype(jnp.int32)
    pl.semaphore_wait(barrier, count)


def remote(src, dst, send_sem, recv_sem, device):
    return pltpu.make_async_remote_copy(
        src_ref=src, dst_ref=dst, send_sem=send_sem, recv_sem=recv_sem,
        device_id=device, device_id_type=pl.DeviceIdType.MESH,
    )


def gather_kernel(
    table, x_hbm, gain_ref, w_hbm, ck_hbm, cv_hbm, ow_hbm,
    proj_ref, kv_ref, og_ref,
    xin, xsub, nsub, turn, grid, wall, row_kv, up, down, own, pout, p_far, p_close,
    load_sem, w_recv, zw_send, o_recv, o_send, zo_send,
    i_recv, i_send, j_recv, j_send, y_recv, y_send, e_recv, e_send,
    c_recv, c_send, m_recv, m_send, f_recv, f_send, r_recv, r_send, s_recv, s_send,
):
    me = lax.axis_index("seq")
    mp = lax.axis_index("mp")
    z, x = me // NX, me % NX
    y, zh, core = mp // 4, (mp // 2) % 2, mp % 2
    right, left, opp = (x + 1) % NX, (x + 3) % NX, (x + 2) % NX
    y_up, y_dn, y_opp = (y + 1) % 4, (y + 3) % 4, (y + 2) % 4
    shard = w_hbm.shape[1]
    tok = xin.shape[0]
    sub = tok // 8
    o_half = og_ref.shape[1] // 2
    peers = (right, left, opp)

    def sub_rows(yc, cc, h=None):
        start = (yc * 2 + cc) * sub
        if h is None:
            return pl.ds(pl.multiple_of(start, sub), sub)
        return pl.ds(pl.multiple_of(start + h * (sub // 2), sub // 2), sub // 2)

    def wrows(zs, k):
        return wall.at[k, pl.ds(pl.multiple_of(zs * shard, 16), shard), :]

    def orows(s, part):
        return og_ref.at[s, pl.ds(part * o_half, o_half), :]

    loads = [
        pltpu.make_async_copy(w_hbm, wall.at[:, pl.ds(pl.multiple_of(z * shard, 16), shard), :], load_sem.at[0]),
        pltpu.make_async_copy(x_hbm.at[sub_rows(y, core), :], xsub, load_sem.at[1]),
        pltpu.make_async_copy(ck_hbm, row_kv.at[0, x], load_sem.at[2]),
        pltpu.make_async_copy(x_hbm, xin, load_sem.at[3]),
        pltpu.make_async_copy(cv_hbm, row_kv.at[1, x], load_sem.at[4]),
        pltpu.make_async_copy(ow_hbm, og_ref.at[me], load_sem.at[5]),
    ]
    for load in loads:
        load.start()

    greet(
        [
            seq_dev(z, right), seq_dev(z, left), seq_dev(jnp.minimum(z + 1, NZ - 1), x), seq_dev(jnp.maximum(z - 1, 0), x),
            mp_dev(y_up, zh, core), mp_dev(y_dn, zh, core), mp_dev(y, zh, 1 - core),
        ],
        [None, None, z < NZ - 1, z > 0, None, None, None],
    )

    def order(j):
        zz = jnp.where(z < 2, z, 3 - z)
        o = zz if j == 0 else (1 - zz if j == 1 else j)
        return jnp.where(z < 2, o, 3 - o)

    def w_copy(j, k, send, device):
        zs = order(j)
        return remote(wrows(zs, k), wrows(zs, k), send, w_recv.at[zs, k], device)

    def o_copy(s, part, send, device):
        return remote(orows(s, part), orows(s, part), send, o_recv.at[s, part], device)

    def oz_copy(j, part, send, device):
        return o_copy(order(j) * NX + x, part, send, device)

    def z_each(j, act):
        zs = order(j)
        for way in (0, 1):
            zt = z + 1 if way == 0 else z - 1
            inside = (zt >= 0) & (zt < NZ)
            if j > 0:
                inside = inside & ((zs < z) if way == 0 else (zs > z))

            @pl.when(inside)
            def _():
                act(way, seq_dev(zt, x))

    def z_start(copy, sends, j, parts):
        z_each(j, lambda way, device: [copy(j, p, sends.at[j, p, way], device).start() for p in parts])

    def z_finish(copy, sends, parts):
        for j in range(NZ):
            z_each(j, lambda way, device: [copy(j, p, sends.at[j, p, way], device).wait_send() for p in parts])

    def z_arrive(copy, sends, j, parts):
        for p in parts:
            copy(j, p, sends.at[j, p, 0], seq_dev(z, right)).wait_recv()

    def w_step(j, k):
        z_arrive(w_copy, zw_send, j, (k,))
        z_start(w_copy, zw_send, j, (k,))

    def x_own(j):
        s = order(j) * NX + x
        for part in (0, 1):
            o_copy(s, part, o_send.at[j, part, 0], seq_dev(z, right)).start()
            o_copy(s, part, o_send.at[j, part, 1], seq_dev(z, left)).start()

    def x_near(j):
        row = order(j) * NX
        for part in (0, 1):
            source, target = (left, right) if part == 0 else (right, left)
            o_copy(row + source, part, o_send.at[j, part, 2], seq_dev(z, target)).wait_recv()
            o_copy(row + source, part, o_send.at[j, part, 2], seq_dev(z, target)).start()
        for part in (0, 1):
            o_copy(row + (right if part == 0 else left), part, o_send.at[j, part, 2], seq_dev(z, right)).wait_recv()

    def x_far(j):
        for part in (0, 1):
            o_copy(order(j) * NX + opp, part, o_send.at[j, part, 2], seq_dev(z, right)).wait_recv()

    def x_finish():
        for j in range(NZ):
            row = order(j) * NX
            for part in (0, 1):
                o_copy(row + x, part, o_send.at[j, part, 0], seq_dev(z, right)).wait_send()
                o_copy(row + x, part, o_send.at[j, part, 1], seq_dev(z, left)).wait_send()
                source = left if part == 0 else right
                o_copy(row + source, part, o_send.at[j, part, 2], seq_dev(z, right)).wait_send()

    def c_copy(kind, xs, way):
        return remote(
            row_kv.at[kind, xs], row_kv.at[kind, xs],
            c_send.at[kind, way, 0 if xs is x else 1], c_recv.at[kind, xs],
            seq_dev(z, right if way == 0 else left),
        )

    half = sub // 2

    def far_in(way):
        target = right if way == 0 else left
        return remote(
            nsub.at[opp, pl.ds(way * half, half)], turn.at[way], i_send.at[way], i_recv.at[way], seq_dev(z, target)
        )

    def pass_in(way):
        source, target = (left, right) if way == 0 else (right, left)
        return remote(
            turn.at[way], grid.at[source, sub_rows(y, core, way)], j_send.at[way], j_recv.at[way], seq_dev(z, target)
        )

    def near_in(way):
        target = right if way == 0 else left
        return remote(
            nsub.at[target], grid.at[x, sub_rows(y, core)], i_send.at[2 + way], i_recv.at[2 + way], seq_dev(z, target)
        )

    def y_copy(xs, yc, h, slot, target):
        ref = grid.at[xs, sub_rows(yc, core, h)]
        return remote(ref, ref, y_send.at[xs, h, slot], y_recv.at[xs, yc, h], mp_dev(target, zh, core))

    def e_copy(xs, yc, cc):
        ref = grid.at[xs, sub_rows(yc, cc)]
        return remote(ref, ref, e_send.at[xs, yc], e_recv.at[xs, yc], mp_dev(y, zh, 1 - core))

    def normed(block):
        wide = block.astype(F32)
        mean = jnp.mean(wide * wide, axis=-1, keepdims=True)
        return (wide * lax.rsqrt(mean + EPS) * gain_ref[...]).astype(BF16)

    def quarter(ref_slot, rows, value, q):
        for zs in range(NZ):
            c = (zs * NX + q) * shard
            grid_or_sub, slot = ref_slot
            grid_or_sub[slot, rows, zs * shard:(zs + 1) * shard] = value[:, c:c + shard]

    loads[0].wait()
    z_start(w_copy, zw_send, 0, (1, 2))
    loads[1].wait()

    @pl.loop(0, sub // 16)
    def _(i):
        rows = pl.ds(pl.multiple_of(i * 16, 16), 16)
        value = normed(xsub[rows, :])
        for q in range(NX):
            quarter((nsub, q), rows, value, q)

    far_in(0).start()
    far_in(1).start()
    near_in(0).start()
    near_in(1).start()
    loads[2].wait()
    c_copy(0, x, 0).start()
    c_copy(0, x, 1).start()
    loads[3].wait()
    for q in range(NX):

        @pl.when(x == q)
        def _():
            @pl.loop(0, tok // 16)
            def _(i):
                rows = pl.ds(pl.multiple_of(i * 16, 16), 16)
                quarter((grid, q), rows, normed(xin[rows, :]), q)

    for way in (0, 1):
        far_in(way).wait_recv()
        pass_in(way).start()
    loads[4].wait()
    c_copy(1, x, 0).start()
    c_copy(1, x, 1).start()
    w_step(1, 1)
    z_start(w_copy, zw_send, 0, (0,))
    for way, xs in ((0, left), (1, right)):
        near_in(way).wait_recv()
        for h in (0, 1):
            y_copy(xs, y, h, 0, y_up).start()
            y_copy(xs, y, h, 1, y_dn).start()
        e_copy(xs, y, core).start()
    for kind in (0, 1):
        source = left if kind == 0 else right
        c_copy(kind, source, kind).wait_recv()
        c_copy(kind, source, kind).start()
    w_step(2, 1)
    w_step(1, 2)
    for way in (0, 1):
        pass_in(way).wait_recv()
        y_copy(opp, y, way, 0, y_up).start()
        y_copy(opp, y, way, 1, y_dn).start()
    e_copy(opp, y, core).start()
    for xs in (left, right, opp):
        for h in (0, 1):
            source, target = (y_dn, y_up) if h == 0 else (y_up, y_dn)
            y_copy(xs, source, h, 2, target).wait_recv()
            y_copy(xs, source, h, 2, target).start()
        for h in (0, 1):
            y_copy(xs, y_up if h == 0 else y_dn, h, 2, y_up).wait_recv()
        e_copy(xs, y_dn, core).start()
        e_copy(xs, y_up, core).start()
    for kind in (0, 1):
        c_copy(kind, right if kind == 0 else left, 0).wait_recv()
    for kind in (0, 1):
        c_copy(kind, opp, 0).wait_recv()

    def held(kind, d, i):
        return row_kv[kind, table[8 + 2 * d + i] // 2, table[8 + 2 * d + i] % 2]

    def message(buffer, way, d, kind):
        return remote(
            buffer.at[d, kind], buffer.at[d, kind], m_send.at[way, d, kind], m_recv.at[way, d, kind],
            seq_dev(jnp.clip(z + 1 - 2 * way, 0, NZ - 1), x),
        )

    def relay(way, hop):
        buffer = up if way == 0 else down
        here = hop if way == 0 else NZ - 1 - hop

        @pl.when(z == here)
        def _():
            passing = range(NZ - 1, here, -1) if way == 0 else range(0, here)
            for d in passing:
                for kind in (0, 1):
                    if hop > 0:
                        message(buffer, way, d, kind).wait_recv()
                    for i in (0, 1):
                        if hop == 0:
                            buffer[d, kind, i] = held(kind, d, i)
                        else:
                            buffer[d, kind, i] = jnp.where(
                                table[2 * d + i] == here, held(kind, d, i), buffer[d, kind, i]
                            )
                    message(buffer, way, d, kind).start()
            if hop > 0:
                for kind in (0, 1):
                    message(buffer, way, here, kind).wait_recv()

    def relay_finish(way):
        buffer = up if way == 0 else down
        for here in range(NZ):
            passing = range(NZ - 1, here, -1) if way == 0 else range(0, here)

            @pl.when(z == here)
            def _():
                for d in passing:
                    for kind in (0, 1):
                        message(buffer, way, d, kind).wait_send()

    p_half = tok // 2

    def p_far_copy(k, way):
        return remote(
            pout.at[k, opp, pl.ds(way * p_half, p_half)], p_far.at[k, way], r_send.at[k, way], r_recv.at[k, way],
            seq_dev(z, right if way == 0 else left),
        )

    def p_close_copy(k, way, h):
        target = right if way == 0 else left
        rows = pl.ds(h * p_half, p_half)
        return remote(
            pout.at[k, target, rows], p_close.at[k, way, rows], s_send.at[k, way, h], s_recv.at[k, way, h],
            seq_dev(z, target),
        )

    def product(k, xs, keep):
        @pl.loop(0, tok // 128)
        def _(i):
            rows = pl.ds(pl.multiple_of(i * 128, 128), 128)
            got = jnp.dot(grid[xs, rows, :], wall[k], preferred_element_type=F32)
            if keep:
                own[k, rows, :] = got
            else:
                pout[k, xs, rows, :] = got.astype(BF16)

    def multiply(k):
        product(k, opp, False)
        p_far_copy(k, 0).start()
        p_far_copy(k, 1).start()
        product(k, right, False)
        p_close_copy(k, 0, 1).start()
        product(k, left, False)
        p_close_copy(k, 1, 0).start()
        product(k, x, True)

    def combine(k):
        for way in (0, 1):
            target = right if way == 0 else left
            rows = pl.ds(way * p_half, p_half)
            p_far_copy(k, way).wait_recv()
            pout[k, target, rows, :] = (
                pout[k, target, rows, :].astype(F32) + p_far[k, way].astype(F32)
            ).astype(BF16)
            p_close_copy(k, way, way).start()

    def collect(k):
        for way in (0, 1):
            for h in (0, 1):
                p_close_copy(k, way, h).wait_recv()
        proj_ref[k] = (own[k] + p_close[k, 0].astype(F32) + p_close[k, 1].astype(F32)).astype(BF16)

    relay(0, 0)
    relay(1, 0)
    loads[5].wait()
    z_start(oz_copy, zo_send, 0, (0, 1))
    x_own(0)
    w_step(3, 1)
    w_step(2, 2)
    w_step(1, 0)
    for xs in (left, right, opp):
        for h in (0, 1):
            y_copy(xs, y_opp, h, 2, y_up).wait_recv()
        e_copy(xs, y_opp, core).start()
    for xs in (left, right, opp):
        for yc in range(4):
            e_copy(xs, yc, 1 - core).wait_recv()
    relay(0, 1)
    relay(1, 1)
    multiply(1)
    w_step(3, 2)
    w_step(2, 0)
    combine(1)
    relay(0, 2)
    relay(1, 2)
    multiply(2)
    w_step(3, 0)
    combine(2)
    relay(0, 3)
    relay(1, 3)
    multiply(0)

    for kind in (0, 1):
        for i in (0, 1):
            low = up[z, kind, i]
            high = down[z, kind, i]
            origin = table[2 * z + i]
            kv_ref[kind, 2 * x + i] = jnp.where(
                origin == z, held(kind, z, i), jnp.where(origin < z, low, high)
            )

    def f_copy(kind, xs, slot, target):
        ref = kv_ref.at[kind, pl.ds(2 * xs, 2)]
        return remote(ref, ref, f_send.at[kind, slot], f_recv.at[kind, xs], seq_dev(z, target))

    for kind in (0, 1):
        f_copy(kind, x, 0, right).start()
        f_copy(kind, x, 1, left).start()
    combine(0)
    for j in (1, 2, 3):
        z_arrive(oz_copy, zo_send, j, (0, 1))
        z_start(oz_copy, zo_send, j, (0, 1))
        x_own(j)
    for kind in (0, 1):
        source, target = (left, right) if kind == 0 else (right, left)
        f_copy(kind, source, 2, target).wait_recv()
        f_copy(kind, source, 2, target).start()
    for j in range(NZ):
        x_near(j)
    for k in (1, 2, 0):
        collect(k)
    for kind in (0, 1):
        f_copy(kind, right if kind == 0 else left, 2, right).wait_recv()
        f_copy(kind, opp, 2, right).wait_recv()
    for j in range(NZ):
        x_far(j)

    for way in (0, 1):
        far_in(way).wait_send()
        pass_in(way).wait_send()
        near_in(way).wait_send()
    for xs in (left, right, opp):
        for h in (0, 1):
            for slot in range(3):
                y_copy(xs, y, h, slot, y_up).wait_send()
        for yc in range(4):
            e_copy(xs, yc, core).wait_send()
    for k in range(3):
        for way in (0, 1):
            p_far_copy(k, way).wait_send()
            for h in (0, 1):
                p_close_copy(k, way, h).wait_send()
    for kind in (0, 1):
        for way in (0, 1):
            c_copy(kind, x, way).wait_send()
        c_copy(kind, left if kind == 0 else right, kind).wait_send()
        for slot in range(3):
            f_copy(kind, x, slot, right).wait_send()
    relay_finish(0)
    relay_finish(1)
    z_finish(w_copy, zw_send, (0, 1, 2))
    z_finish(oz_copy, zo_send, (0, 1))
    x_finish()


def attend_kernel(
    length, proj_ref, kv_ref, og_ref, out_ref,
    near, top, total, mixed, attended, parts, mates, ring, sums,
    k_recv, k_send, a_recv, a_send, y_recv, y_send, h_recv, h_send,
):
    me = lax.axis_index("seq")
    mp = lax.axis_index("mp")
    z, x = me // NX, me % NX
    right, left, opp = (x + 1) % NX, (x + 3) % NX, (x + 2) % NX
    y, zh, core = mp // 4, (mp // 2) % 2, mp % 2
    y_up, y_dn, y_opp = (y + 1) % 4, (y + 3) % 4, (y + 2) % 4
    tok = proj_ref.shape[1]

    greet(
        [seq_dev(z, right), seq_dev(z, left), mp_dev(y, zh, 1 - core), mp_dev(y_up, zh, core), mp_dev(y_dn, zh, core), mp_dev(y, 1 - zh, core)],
        [None] * 6,
    )

    def k_copy(kind, xs, slot, target):
        src = proj_ref.at[1 + kind] if xs is x else near.at[kind, xs]
        return remote(src, near.at[kind, xs], k_send.at[kind, slot], k_recv.at[kind, xs], seq_dev(z, target))

    for kind in (0, 1):
        k_copy(kind, x, 0, right).start()
        k_copy(kind, x, 1, left).start()

    scale = HD ** (-0.5)

    def update(keys, values, mask, first=False):
        scores = lax.dot_general(
            proj_ref[0], keys, (((1,), (1,)), ((), ())), preferred_element_type=F32
        ) * scale
        if mask is not None:
            scores = jnp.where(mask, scores, LOWEST)
        largest = jnp.max(scores, axis=-1, keepdims=True)
        if not first:
            largest = jnp.maximum(largest, top[...])
        weights = jnp.exp(scores - largest)
        weight_sum = jnp.sum(weights, axis=-1, keepdims=True)
        got = jnp.dot(weights.astype(BF16), values, preferred_element_type=F32)
        if first:
            total[...] = weight_sum
            mixed[...] = got
        else:
            fade = jnp.exp(top[...] - largest)
            total[...] = total[...] * fade + weight_sum
            mixed[...] = mixed[...] * fade + got
        top[...] = largest

    columns = lax.broadcasted_iota(jnp.int32, (tok, 512), 1)
    update(
        kv_ref[0, 0:2].reshape(512, HD), kv_ref[1, 0:2].reshape(512, HD), columns < length[0], True
    )

    @pl.loop(1, 4)
    def _(c):
        two = pl.ds(2 * c, 2)
        ids = lax.broadcasted_iota(jnp.int32, (tok, 512), 1) + c * 512
        update(kv_ref[0, two].reshape(512, HD), kv_ref[1, two].reshape(512, HD), ids < length[0])

    rows = lax.broadcasted_iota(jnp.int32, (tok, tok), 0)
    update(proj_ref[1], proj_ref[2], columns <= rows)

    for kind in (0, 1):
        source, target = (left, right) if kind == 0 else (right, left)
        k_copy(kind, source, 2, target).wait_recv()
        k_copy(kind, source, 2, target).start()
    for kind in (0, 1):
        k_copy(kind, right if kind == 0 else left, 2, right).wait_recv()

    @pl.when(x > 0)
    def _():
        update(near[0, left], near[1, left], None)

    @pl.when(x == NX - 1)
    def _():
        update(near[0, right], near[1, right], None)

    for kind in (0, 1):
        k_copy(kind, opp, 2, right).wait_recv()

    @pl.when(x > 1)
    def _():
        update(near[0, opp], near[1, opp], None)

    attended[...] = (mixed[...] / total[...]).astype(BF16)

    @pl.loop(0, 8)
    def _(c):
        parts[c] = jnp.dot(
            attended[...], og_ref[2 * c + 1 - core], preferred_element_type=F32
        ).astype(BF16)

    mate = remote(parts, mates, a_send, a_recv, mp_dev(y, zh, 1 - core))
    mate.start()

    @pl.loop(0, 8)
    def _(c):
        sums[c] = jnp.dot(attended[...], og_ref[2 * c + core], preferred_element_type=F32).astype(BF16)

    mate.wait_recv()

    @pl.loop(0, 8)
    def _(c):
        sums[c] = (sums[c].astype(F32) + mates[c].astype(F32)).astype(BF16)

    def far(way):
        target = y_up if way == 0 else y_dn
        return remote(
            sums.at[2 * y_opp + way], ring.at[way, 0], y_send.at[way, 0], y_recv.at[way, 0],
            mp_dev(target, zh, core),
        )

    def close(way, h):
        target = y_up if way == 0 else y_dn
        return remote(
            sums.at[2 * target + h], ring.at[way, 1 + h], y_send.at[way, 1 + h], y_recv.at[way, 1 + h],
            mp_dev(target, zh, core),
        )

    far(0).start()
    far(1).start()
    for way in (0, 1):
        close(way, 1 - way).start()
    for way in (0, 1):
        target = y_up if way == 0 else y_dn
        far(way).wait_recv()
        sums[2 * target + way] = (
            sums[2 * target + way].astype(F32) + ring[way, 0].astype(F32)
        ).astype(BF16)
        close(way, way).start()
    for way in (0, 1):
        for h in (0, 1):
            close(way, h).wait_recv()

    def chunk(h):
        return sums[2 * y + h].astype(F32) + ring[0, 1 + h].astype(F32) + ring[1, 1 + h].astype(F32)

    attended[...] = jnp.where(zh == 0, chunk(1), chunk(0)).astype(BF16)
    last = remote(attended, near.at[0, x], h_send, h_recv, mp_dev(y, 1 - zh, core))
    last.start()
    mine = jnp.where(zh == 0, chunk(0), chunk(1))
    last.wait_recv()
    out_ref[...] = (mine + near[0, x].astype(F32)).astype(BF16)

    for kind in (0, 1):
        for slot in range(3):
            k_copy(kind, x, slot, right).wait_send()
    mate.wait_send()
    for way in (0, 1):
        far(way).wait_send()
        close(way, 0).wait_send()
        close(way, 1).wait_send()
    last.wait_send()


def vmem():
    return pl.BlockSpec(memory_space=pltpu.VMEM)


def smem():
    return pl.BlockSpec(memory_space=pltpu.SMEM)


def hbm():
    return pl.BlockSpec(memory_space=pl.ANY)


def per_device(
    inputs, norm_gain, qkv_weight, adapter_down, adapter_up, out_weight,
    cache_keys, cache_values, cache_lengths, block_perm,
):
    tok, d_in = inputs.shape
    shard = qkv_weight.shape[0]
    blk = cache_keys.shape[1]
    dma = pltpu.SemaphoreType.DMA
    me = lax.axis_index("seq")
    z, x = me // NX, me % NX

    folded = (
        qkv_weight.transpose(1, 0, 2).astype(F32)
        + jnp.einsum("rj,kjc->krc", adapter_down, adapter_up, preferred_element_type=F32)
    ).astype(BF16)

    logical = jnp.arange(NZ, dtype=jnp.int32)[:, None] * 8 + 2 * x + jnp.arange(2, dtype=jnp.int32)[None, :]
    count = block_perm.shape[0]
    hits = block_perm[None, :] == logical.reshape(-1)[:, None]
    place = jnp.sum(jnp.where(hits, jnp.arange(count, dtype=jnp.int32)[None, :], 0), axis=-1)
    table = jnp.concatenate([place // 8, place % 8]).astype(jnp.int32)
    length = jnp.sum(
        jnp.where(jnp.arange(REQS, dtype=jnp.int32) == z, cache_lengths, 0)
    ).reshape(1)

    proj, kv, og = pl.pallas_call(
        gather_kernel,
        out_shape=(
            jax.ShapeDtypeStruct((3, tok, HD), BF16),
            jax.ShapeDtypeStruct((2, 8, blk, HD), BF16),
            jax.ShapeDtypeStruct((16, HD, HD), BF16),
        ),
        in_specs=[smem(), hbm(), vmem(), hbm(), hbm(), hbm(), hbm()],
        out_specs=(vmem(), vmem(), vmem()),
        scratch_shapes=[
            pltpu.VMEM((tok, d_in), BF16),
            pltpu.VMEM((tok // 8, d_in), BF16),
            pltpu.VMEM((NX, tok // 8, d_in // NX), BF16),
            pltpu.VMEM((2, tok // 16, d_in // NX), BF16),
            pltpu.VMEM((NX, tok, d_in // NX), BF16),
            pltpu.VMEM((3, d_in // NX, HD), BF16),
            pltpu.VMEM((2, NX, 2, blk, HD), BF16),
            pltpu.VMEM((NZ, 2, 2, blk, HD), BF16),
            pltpu.VMEM((NZ, 2, 2, blk, HD), BF16),
            pltpu.VMEM((3, tok, HD), F32),
            pltpu.VMEM((3, NX, tok, HD), BF16),
            pltpu.VMEM((3, 2, tok // 2, HD), BF16),
            pltpu.VMEM((3, 2, tok, HD), BF16),
            dma((6,)), dma((4, 3)), dma((4, 3, 2)),
            dma((16, 2)), dma((4, 2, 3)), dma((4, 2, 2)),
            dma((4,)), dma((4,)), dma((2,)), dma((2,)),
            dma((4, 4, 2)), dma((4, 2, 3)), dma((4, 4)), dma((4, 4)),
            dma((2, 4)), dma((2, 2, 2)),
            dma((2, 4, 2)), dma((2, 4, 2)),
            dma((2, 4)), dma((2, 3)),
            dma((3, 2)), dma((3, 2)), dma((3, 2, 2)), dma((3, 2, 2)),
        ],
        compiler_params=pltpu.CompilerParams(
            collective_id=0, has_side_effects=True, vmem_limit_bytes=VMEM_LIMIT
        ),
        name="gather",
    )(table, inputs, norm_gain.reshape(1, d_in), folded, cache_keys, cache_values, out_weight)

    return pl.pallas_call(
        attend_kernel,
        out_shape=jax.ShapeDtypeStruct((tok, HD), BF16),
        in_specs=[smem(), vmem(), vmem(), vmem()],
        out_specs=vmem(),
        scratch_shapes=[
            pltpu.VMEM((2, NX, tok, HD), BF16),
            pltpu.VMEM((tok, 1), F32),
            pltpu.VMEM((tok, 1), F32),
            pltpu.VMEM((tok, HD), F32),
            pltpu.VMEM((tok, HD), BF16),
            pltpu.VMEM((8, tok, HD), BF16),
            pltpu.VMEM((8, tok, HD), BF16),
            pltpu.VMEM((2, 3, tok, HD), BF16),
            pltpu.VMEM((8, tok, HD), BF16),
            dma((2, 4)), dma((2, 3)),
            dma, dma,
            dma((2, 3)), dma((2, 3)),
            dma, dma,
        ],
        compiler_params=pltpu.CompilerParams(
            collective_id=1, has_side_effects=True, vmem_limit_bytes=VMEM_LIMIT
        ),
        name="attend",
    )(length, proj, kv, og)


def solution(mesh):
    in_specs = (
        P("seq", None), P(), P("seq", None, "mp"), P("seq", None), P(None, None, "mp"),
        P("mp", "seq"), P("seq", None, "mp"), P("seq", None, "mp"), P(), P(),
    )
    return jax.shard_map(
        per_device, mesh=mesh, in_specs=in_specs, out_specs=P("seq", "mp"), check_vma=False
    )
```
